128 devices in a mesh: row: 16 (over y, x), col: 8 (over z, core).
Axes of the slice: x: 4, y: 4, z: 4, core: 2. Of those that a mesh axis runs over, the one named last changes fastest.
Arguments:
- ancestor_inverse: float32 [20480, 20480], P('row', 'col'), may hold values from -0.3125 to 0.3125
- panel_parent: float32 [20480, 512], P('row'), may hold values from -0.5 to 0.5
- panel_child: float32 [20480, 512], P('row'), may hold values from -0.5 to 0.5
- coupling: float32 [512, 512], replicated, may hold values from -0.125 to 0.125
- diag_parent: float32 [512, 512], replicated, may hold values from -3 to 3
- diag_child: float32 [512, 512], replicated, may hold values from -3 to 3
- structure: int32 [2, 160], replicated, may hold values from 0 to 1, as said below
Outputs:
- parent_rows: float32 [20480, 512], P(('row', 'col'))
- parent_diag: float32 [512, 512], P(('row', 'col'))
- child_top: float32 [512, 512], P(('row', 'col'))
- child_rows: float32 [20480, 512], P(('row', 'col'))
- child_diag: float32 [512, 512], P(('row', 'col'))
The draws below stay inside these ranges and needn't reach their ends.
Inputs may be any that keep to these rules, and one draw needn't show every extreme that they name: `structure`: every entry is a flag of one block of 128 ancestor rows; a block flagged in row 1 is flagged in row 0, and the last block is flagged in both rows.
All inputs are finite; a program needn't handle non-finite values.
Results may differ from the reference program's by a relative error of at most 0.00007.
Values sent between devices are 32-bit elements; how exact they have to be, the bound alone decides.
No kernel may reach another device: no remote copies, remote signals or barrier semaphores. Data moves between devices by JAX's collectives and lax.ppermute only.
A program may use at most 128 MiB of HBM per device.

```python
import jax
import jax.numpy as jnp
from jax import lax

W = 512
BLK = 128
NR = 20480
NB = 160


def draw_structure(key, part):
    base = jax.random.fold_in(key, 17)
    key_parent = jax.random.fold_in(base, 1)
    key_child = jax.random.fold_in(base, 2)
    blocks = jnp.arange(NB, dtype=jnp.int32)
    threshold = 20 + 70 * blocks // NB
    rolled = jax.random.randint(key_parent, (NB,), 0, 100, dtype=jnp.int32)
    parent = (rolled < threshold).astype(jnp.int32)
    parent = jnp.where(blocks == NB - 1, 1, parent)
    halves = jax.random.randint(key_child, (NB,), 0, 2, dtype=jnp.int32)
    child = parent * halves
    child = jnp.where(blocks == NB - 1, 1, child)
    return jnp.stack([parent, child]).astype(jnp.int32)


def steps_of(own_key, shape, cuts, low, largest):
    def one(axis_at, blocks):
        steps = jax.random.uniform(jax.random.fold_in(jax.random.fold_in(own_key, 6), axis_at), (blocks,), jnp.float32, low / len(cuts), largest / len(cuts))
        return jnp.repeat(jnp.exp(steps), shape[axis_at] // blocks).reshape((-1,) + (1,) * (len(shape) - axis_at - 1))

    level = one(*cuts[0])
    for cut in cuts[1:]:
        level = level * one(*cut)
    return level


def bell_draw(own_key, dims, deviation, most, split=(), kind=jnp.bfloat16):
    array = jax.random.normal(own_key, dims, jnp.float32) * deviation
    if len(split) > 0:
        array = steps_of(own_key, dims, split, -0.22, 0.18) * array
    return jnp.clip(array, min=-most, max=most).astype(kind)


def setup_inputs(seed: int = 0) -> dict:
    keys = jax.random.split(jax.random.key(seed), 8)
    ancestor_inverse = bell_draw(keys[0], (NR, NR), (NR // 64) ** -0.5, 0.3125, ((0, 16), (1, 8)), jnp.float32)
    panel_parent = bell_draw(keys[1], (NR, W), 0.0625, 0.5, ((0, 16),), jnp.float32)
    panel_child = bell_draw(keys[2], (NR, W), 0.0625, 0.5, ((0, 16),), jnp.float32)
    coupling = bell_draw(keys[3], (W, W), (4 * W) ** -0.5, 0.125, (), jnp.float32)
    diag_parent = bell_draw(keys[4], (W, W), 0.5, 3.0, (), jnp.float32)
    diag_child = bell_draw(keys[5], (W, W), 0.5, 3.0, (), jnp.float32)
    structure = draw_structure(jax.random.fold_in(keys[7], 71), 0)
    return {"ancestor_inverse": ancestor_inverse, "panel_parent": panel_parent, "panel_child": panel_child, "coupling": coupling, "diag_parent": diag_parent, "diag_child": diag_child, "structure": structure}


def product(left, right):
    return jnp.dot(left, right, precision=lax.Precision.HIGHEST, preferred_element_type=jnp.float32)


def reference(ancestor_inverse, panel_parent, panel_child, coupling, diag_parent, diag_child, structure):
    mask_parent = jnp.repeat(structure[0], BLK).astype(jnp.float32)[:, None]
    mask_child = jnp.repeat(structure[1], BLK).astype(jnp.float32)[:, None]
    parent = panel_parent * mask_parent
    child = panel_child * mask_child
    parent_prod = product(ancestor_inverse, parent)
    parent_rows = -parent_prod * mask_parent
    parent_diag = diag_parent + product(parent.T, parent_prod)
    top_prod = product(parent_diag, coupling) + product(parent_rows.T, child)
    rows_prod = product(parent_rows, coupling) + product(ancestor_inverse, child)
    child_top = -top_prod
    child_rows = -rows_prod * mask_child
    child_diag = diag_child + product(coupling.T, top_prod) + product(child.T, rows_prod)
    return parent_rows, parent_diag, child_top, child_rows, child_diag
```

```python
import functools

import jax
import jax.numpy as jnp
from jax import lax
from jax.experimental import pallas as pl
from jax.experimental.pallas import tpu as pltpu
from jax.sharding import PartitionSpec as P

BLK = 128
SUB = 8
SIDE = 4
CORES = 2
RING = SIDE * SIDE
TILE_BLOCKS = 10
COL_BLOCKS = 20
W = 512
AXES = ("row", "col")


def device(y, x, z, core):
    return ((y % SIDE) * SIDE + x % SIDE) * SIDE * CORES + (z % SIDE) * CORES + core


def pairs(target):
    return [
        (device(y, x, z, core), device(*target(y, x, z, core)))
        for y in range(SIDE)
        for x in range(SIDE)
        for z in range(SIDE)
        for core in range(CORES)
    ]


STEPS = {
    "y": lambda by: pairs(lambda y, x, z, core: (y + by, x, z, core)),
    "x": lambda by: pairs(lambda y, x, z, core: (y, x + by, z, core)),
    "z": lambda by: pairs(lambda y, x, z, core: (y, x, z + by, core)),
}
PARTNER = pairs(lambda y, x, z, core: (y, x, z, 1 - core))
SPREAD = [
    pairs(lambda y, x, z, core: (z, 2 * core + (x + flip) % 2, y, x // 2)) for flip in range(2)
]


def shift(value, axis, by):
    return lax.ppermute(value, AXES, STEPS[axis](by))


def product(left, right):
    return jnp.dot(left, right, precision=lax.Precision.HIGH, preferred_element_type=jnp.float32)


def product_t(left, right):
    return lax.dot_general(
        left, right, (((0,), (0,)), ((), ())), precision=lax.Precision.HIGH,
        preferred_element_type=jnp.float32,
    )


def compact_body(caps, structure, first, second, *outs):
    col = lax.axis_index("col")
    side = lax.axis_index("row") % 2
    for which in range(2):
        half = caps[which] // 2
        low, high = outs[2 * which], outs[2 * which + 1]

        def step(block, slot):
            flag = structure[which, col * COL_BLOCKS + block]
            part = block // TILE_BLOCKS
            own = block - part * TILE_BLOCKS

            @pl.when(flag == 1)
            def _():
                value = jnp.where(part == side, first[which, own], second[which, own])

                @pl.when(slot < half)
                def _():
                    low[slot] = value

                @pl.when(slot >= half)
                def _():
                    high[slot - half] = value

            return slot + flag

        lax.fori_loop(0, COL_BLOCKS, step, 0)


def compact(caps, structure, first, second):
    vmem = pl.BlockSpec(memory_space=pltpu.VMEM)
    shapes = [jax.ShapeDtypeStruct((cap // 2, SUB, W), jnp.float32) for cap in caps for _ in range(2)]
    return pl.pallas_call(
        functools.partial(compact_body, caps),
        in_specs=[pl.BlockSpec(memory_space=pltpu.SMEM), vmem, vmem],
        out_specs=[vmem] * 4,
        out_shape=shapes,
        name="compact",
    )(structure, first, second)


def gather_stage(own, axis):
    half = own.shape[0] // 2
    before = shift(own, axis, 1)
    after = shift(own, axis, -1)
    far_low = shift(before[:half], axis, 1)
    far_high = shift(after[half:], axis, -1)
    return before, after, far_low, far_high


def plane_gather(share, axes):
    before, after, far_low, far_high = gather_stage(share, axes[0])
    line = jnp.stack([share, after, jnp.concatenate([far_low, far_high]), before])
    return (line, *gather_stage(line, axes[1]))


def split(value):
    high = value.astype(jnp.bfloat16)
    low = (value - high.astype(jnp.float32)).astype(jnp.bfloat16)
    return high, low


def tile_body(which, cap, structure, inverse, *refs):
    lines, (mine, theirs) = refs[:10], refs[10:12]
    columns, rows, tiles, panel, right, acc, panel_sem, tile_sems, out_sem = refs[12:]
    row = lax.axis_index("row")
    col = lax.axis_index("col")
    y, x, z, core = row // SIDE, row % SIDE, col // CORES, col % CORES
    half = cap // 2

    def line_copies():
        copies = []
        for order in range(2):
            own, before, after, far_low, far_high = lines[5 * order : 5 * order + 5]
            pieces = [(own, 0, i, i) for i in range(SIDE)]
            pieces += [(after, 1, i, i) for i in range(SIDE)]
            pieces += [(before, 3, i, i) for i in range(SIDE)]
            pieces += [(far_low, 2, i, i) for i in range(2)]
            pieces += [(far_high, 2, i, i + 2) for i in range(2)]
            for ref, outer, at, inner in pieces:
                if order == 0:
                    sub = (y + outer) % SIDE * SIDE + (x + inner) % SIDE
                else:
                    sub = (y + inner) % SIDE * SIDE + (x + outer) % SIDE
                copies.append(
                    pltpu.make_async_copy(
                        ref.at[at],
                        panel.at[pl.ds(order * half, half), sub],
                        panel_sem.at[len(copies)],
                    )
                )
        return copies

    copies = line_copies()
    for copy in copies:
        copy.start()

    def scan(count, offset, table):
        def step(block, slot):
            flag = structure[which, offset + block]

            @pl.when(flag == 1)
            def _():
                table[slot] = block

            return slot + flag

        return lax.fori_loop(0, count, step, 0)

    slots = scan(COL_BLOCKS, col * COL_BLOCKS, columns)
    lines_used = scan(TILE_BLOCKS, row * TILE_BLOCKS, rows)

    @pl.when(slots % 2 == 1)
    def _():
        columns[slots] = columns[slots - 1]

    @pl.when(lines_used % 2 == 1)
    def _():
        rows[lines_used] = TILE_BLOCKS

    steps = (slots + 1) // 2
    chunks = (lines_used + 1) // 2

    def tile_copy(step, at):
        block = columns[2 * step + at]
        buffer = step % 2
        return pltpu.make_async_copy(
            inverse.at[:, :, pl.ds(block * BLK, BLK)],
            tiles.at[buffer, :, :, pl.ds(at * BLK, BLK)],
            tile_sems.at[buffer, at],
        )

    for ahead in range(2):

        @pl.when(ahead < steps)
        def _():
            tile_copy(ahead, 0).start()
            tile_copy(ahead, 1).start()

    acc[...] = jnp.zeros_like(acc)
    for copy in copies:
        copy.wait()

    @pl.when(slots % 2 == 1)
    def _():
        panel[slots] = jnp.zeros((BLK // SUB, SUB, W), jnp.float32)

    def prepare(step, _):
        value = panel[pl.ds(2 * step, 2)].reshape(2 * BLK, W)
        high, low = split(value)
        right[step, 0 : 2 * BLK] = high
        right[step, 2 * BLK : 4 * BLK] = low
        right[step, 4 * BLK : 6 * BLK] = high
        return 0

    lax.fori_loop(0, steps, prepare, 0)

    def contract(step, _):
        tile_copy(step, 0).wait()
        tile_copy(step, 1).wait()
        buffer = step % 2

        def chunk(at, _):
            above, below = rows[2 * at], rows[2 * at + 1]
            value = jnp.concatenate(
                [tiles[buffer, above], tiles[buffer, jnp.minimum(below, TILE_BLOCKS - 1)]], axis=0
            )
            high, low = split(value)
            left = jnp.concatenate([high, high, low], axis=1)
            part = jnp.dot(left, right[step], preferred_element_type=jnp.float32)
            acc[above] += part[:BLK]
            acc[below] += part[BLK:]
            return 0

        lax.fori_loop(0, chunks, chunk, 0)

        @pl.when(step + 2 < steps)
        def _():
            tile_copy(step + 2, 0).start()
            tile_copy(step + 2, 1).start()

        return 0

    lax.fori_loop(0, steps, contract, 0)

    flat = acc.reshape((TILE_BLOCKS + 1) * BLK, W)
    group = TILE_BLOCKS * BLK // (SIDE * CORES)
    out_copies = []
    for at in range(SIDE):
        level = (z + at) % SIDE
        for ref, side in ((mine, core), (theirs, 1 - core)):
            start = pl.multiple_of((level * CORES + side) * group, 32)
            out_copies.append(
                pltpu.make_async_copy(flat.at[pl.ds(start, group)], ref.at[at], out_sem.at[len(out_copies)])
            )
    for copy in out_copies:
        copy.start()
    for copy in out_copies:
        copy.wait()


def tile_product(which, cap, structure, inverse, lines):
    hbm = pl.BlockSpec(memory_space=pl.ANY)
    group = TILE_BLOCKS * BLK // (SIDE * CORES)
    shape = jax.ShapeDtypeStruct((SIDE, group, W), jnp.float32)
    return pl.pallas_call(
        functools.partial(tile_body, which, cap),
        in_specs=[pl.BlockSpec(memory_space=pltpu.SMEM)] + [hbm] * 11,
        out_specs=[hbm] * 2,
        out_shape=[shape] * 2,
        scratch_shapes=[
            pltpu.SMEM((COL_BLOCKS + 2,), jnp.int32),
            pltpu.SMEM((TILE_BLOCKS + 2,), jnp.int32),
            pltpu.VMEM((2, TILE_BLOCKS, BLK, 2 * BLK), jnp.float32),
            pltpu.VMEM((cap, BLK // SUB, SUB, W), jnp.float32),
            pltpu.VMEM((cap // 2, 6 * BLK, W), jnp.bfloat16),
            pltpu.VMEM((TILE_BLOCKS + 1, BLK, W), jnp.float32),
            pltpu.SemaphoreType.DMA((2 * 16,)),
            pltpu.SemaphoreType.DMA((2, 2)),
            pltpu.SemaphoreType.DMA((8,)),
        ],
        name="tile_product_%d" % which,
    )(structure, inverse.reshape(TILE_BLOCKS, BLK, COL_BLOCKS * BLK), *lines)


def level_sum(mine, theirs):
    chunks = mine + lax.ppermute(theirs, AXES, PARTNER)
    half = chunks.shape[1] // 2
    up = shift(chunks[2, :half], "z", 1)
    down = shift(chunks[2, half:], "z", -1)
    above = jnp.concatenate([chunks[1, :half] + up, chunks[1, half:]])
    below = jnp.concatenate([chunks[3, :half], chunks[3, half:] + down])
    return chunks[0] + shift(above, "z", 1) + shift(below, "z", -1)


def axis_sum(value, axis, index):
    part = value.reshape(SIDE, value.shape[0] // SIDE, *value.shape[1:])

    def piece(at):
        return lax.dynamic_index_in_dim(part, (index + at) % SIDE, 0, keepdims=False)

    got = [shift(piece(at), axis, at) for at in (1, 2, 3)]
    return piece(0) + got[0] + got[1] + got[2]


def spread_sum(value, y, x, z, core):
    pieces = value.reshape(RING * SIDE, CORES, SIDE, value.shape[1])
    theirs = lax.dynamic_index_in_dim(pieces, 1 - core, 1, keepdims=False)
    mine = lax.dynamic_index_in_dim(pieces, core, 1, keepdims=False)
    value = mine + lax.ppermute(theirs, AXES, PARTNER)
    value = axis_sum(value, "y", y)
    value = axis_sum(value, "x", x)
    value = axis_sum(value, "z", z)
    return value[0]


def on_device(
    ancestor_inverse, panel_parent, panel_child, coupling, diag_parent, diag_child, structure
):
    row = lax.axis_index("row")
    col = lax.axis_index("col")
    y, x, z, core = row // SIDE, row % SIDE, col // CORES, col % CORES
    side = row % 2
    caps = (COL_BLOCKS, COL_BLOCKS)
    tile_rows = panel_parent.shape[0]
    group_rows = tile_rows // (SIDE * CORES)
    own_count = W // (RING * SIDE * CORES)
    own_start = (row * SIDE * CORES + col) * own_count

    panels = jnp.stack([panel_parent, panel_child]).reshape(2, TILE_BLOCKS, BLK // SUB, SUB, W)

    def slices(sub):
        return lax.dynamic_index_in_dim(panels, sub, 2, keepdims=False)

    first = lax.ppermute(slices(2 * col + side), AXES, SPREAD[0])
    second = lax.ppermute(slices(2 * col + 1 - side), AXES, SPREAD[1])
    shares = compact(caps, structure, first, second)
    parent_lines = plane_gather(shares[0], "yx"[::-1]) + plane_gather(shares[1], "yx")
    child_lines = plane_gather(shares[2], "yx"[::-1]) + plane_gather(shares[3], "yx")

    block_rows = jnp.arange(tile_rows, dtype=jnp.int32) // BLK

    def group_mask(which):
        flags = lax.dynamic_slice_in_dim(structure[which], row * TILE_BLOCKS, TILE_BLOCKS)
        at = lax.dynamic_slice_in_dim(block_rows, col * group_rows, group_rows)
        hits = (at[:, None] == jnp.arange(TILE_BLOCKS, dtype=jnp.int32)[None, :]) & (flags[None, :] == 1)
        return jnp.any(hits, axis=1)[:, None].astype(jnp.float32)

    def group_of(values):
        return lax.dynamic_slice_in_dim(values, col * group_rows, group_rows, 0)

    mask_parent, mask_child = group_mask(0), group_mask(1)
    parent = group_of(panel_parent) * mask_parent
    child = group_of(panel_child) * mask_child

    mine, theirs = tile_product(0, caps[0], structure, ancestor_inverse, parent_lines)
    parent_rows = -level_sum(mine, theirs) * mask_parent
    carried = product(parent_rows, coupling)
    parent_term = -product_t(parent, parent_rows)
    mine, theirs = tile_product(1, caps[1], structure, ancestor_inverse, child_lines)
    rows_prod = level_sum(mine, theirs) + carried
    child_rows = -rows_prod * mask_child
    top_term = product(parent_term, coupling) + product_t(parent_rows, child)
    child_term = product_t(coupling, top_term) + product_t(child, rows_prod)
    sums = spread_sum(jnp.concatenate([parent_term, top_term, child_term], axis=1), y, x, z, core)

    def own_rows(values):
        return lax.dynamic_slice_in_dim(values, own_start, own_count, 0)

    base_top = product(diag_parent, coupling)
    coupling_cols = lax.dynamic_slice_in_dim(coupling, own_start, own_count, 1)
    parent_diag = own_rows(diag_parent) + sums[:, :W]
    child_top = -(own_rows(base_top) + sums[:, W : 2 * W])
    child_diag = own_rows(diag_child) + product_t(coupling_cols, base_top) + sums[:, 2 * W :]
    return parent_rows, parent_diag, child_top, child_rows, child_diag


def solution(mesh):
    return jax.shard_map(
        on_device,
        mesh=mesh,
        in_specs=(P("row", "col"), P("row", None), P("row", None), P(), P(), P(), P()),
        out_specs=(P(AXES, None),) * 5,
        check_vma=False,
    )
```

```python
import functools

import jax
import jax.numpy as jnp
from jax import lax
from jax.experimental import pallas as pl
from jax.experimental.pallas import tpu as pltpu
from jax.sharding import PartitionSpec as P

BLK = 128
SUB = 8
SIDE = 4
CORES = 2
RING = SIDE * SIDE
TILE_BLOCKS = 10
COL_BLOCKS = 20
W = 512
AXES = ("row", "col")
CAPS = (20, 20)
CHUNKS = ((0, 4), (4, 7), (7, 10))


def device(y, x, z, core):
    return ((y % SIDE) * SIDE + x % SIDE) * SIDE * CORES + (z % SIDE) * CORES + core


def pairs(target):
    return [
        (device(y, x, z, core), device(*target(y, x, z, core)))
        for y in range(SIDE)
        for x in range(SIDE)
        for z in range(SIDE)
        for core in range(CORES)
    ]


def stepped(axis, by):
    def target(y, x, z, core):
        along = axis[core]
        return y + by * (along == "y"), x + by * (along == "x"), z + by * (along == "z"), core

    return pairs(target)


PARTNER = pairs(lambda y, x, z, core: (y, x, z, 1 - core))


def spread_target(y, x, z, core, flip):
    turn = 2 * core + (x + flip) % 2
    return (y + turn) % SIDE, (x + z + turn) % SIDE, y, x // 2


SPREAD = [
    pairs(lambda y, x, z, core, flip=flip: spread_target(y, x, z, core, flip)) for flip in range(2)
]


def shift(value, axis, by):
    return lax.ppermute(value, AXES, stepped(axis, by))


def product(left, right):
    return jnp.dot(left, right, precision=lax.Precision.HIGH, preferred_element_type=jnp.float32)


def product_t(left, right):
    return lax.dot_general(
        left, right, (((0,), (0,)), ((), ())), precision=lax.Precision.HIGH,
        preferred_element_type=jnp.float32,
    )


def compact_body(caps, structure, first, second, share):
    col = lax.axis_index("col")
    near = (lax.axis_index("row") // SIDE + SIDE - col // CORES) % 2
    for which in range(2):

        def step(block, slot):
            flag = structure[which, col * COL_BLOCKS + block]
            part = block // TILE_BLOCKS
            own = block - part * TILE_BLOCKS

            @pl.when(flag == 1)
            def _():
                share[slot] = jnp.where(part == near, first[which, own], second[which, own])

            return slot + flag

        lax.fori_loop(0, COL_BLOCKS, step, which * caps[0])


def compact(caps, structure, first, second):
    vmem = pl.BlockSpec(memory_space=pltpu.VMEM)
    return pl.pallas_call(
        functools.partial(compact_body, caps),
        in_specs=[pl.BlockSpec(memory_space=pltpu.SMEM), vmem, vmem],
        out_specs=vmem,
        out_shape=jax.ShapeDtypeStruct((sum(caps), SUB, W), jnp.float32),
        name="compact",
    )(structure, first, second)


def gather_near(own, axis):
    return shift(own, axis, 1), shift(own, axis, -1)


def gather_far(before, after, axis):
    half = before.shape[0] // 2
    return shift(before[:half], axis, 1), shift(after[half:], axis, -1)


def gather_line(share, axis):
    before, after = gather_near(share, axis)
    far_low, far_high = gather_far(before, after, axis)
    return share, after, jnp.concatenate([far_low, far_high]), before


def split(value):
    high = value.astype(jnp.bfloat16)
    low = (value - high.astype(jnp.float32)).astype(jnp.bfloat16)
    return high, low


def tile_body(which, cap, structure, inverse, *refs):
    (own, before, after, far_low, far_high), (mine, theirs, whole) = refs[:5], refs[5:8]
    columns, rows, tiles, panel, left, right, acc, panel_sem, tile_sems, out_sem = refs[8:]
    row = lax.axis_index("row")
    col = lax.axis_index("col")
    y, x, z, core = row // SIDE, row % SIDE, col // CORES, col % CORES

    def line_copies():
        copies = []
        pieces = [(own, 0, i, i) for i in range(SIDE)]
        pieces += [(after, 1, i, i) for i in range(SIDE)]
        pieces += [(before, 3, i, i) for i in range(SIDE)]
        pieces += [(far_low, 2, i, i) for i in range(2)]
        pieces += [(far_high, 2, i, i + 2) for i in range(2)]
        for ref, outer, at, inner in pieces:
            sub_y = (y + jnp.where(core == 0, outer, inner)) % SIDE
            sub_x = (x + jnp.where(core == 0, inner, outer)) % SIDE
            copies.append(
                pltpu.make_async_copy(
                    ref.at[at], panel.at[:, sub_y * SIDE + sub_x], panel_sem.at[len(copies)]
                )
            )
        return copies

    copies = line_copies()
    for copy in copies:
        copy.start()

    def scan(count, offset, table):
        def step(block, slot):
            flag = structure[which, offset + block]

            @pl.when(flag == 1)
            def _():
                table[slot] = block

            return slot + flag

        return lax.fori_loop(0, count, step, 0)

    slots = scan(COL_BLOCKS, col * COL_BLOCKS, columns)
    lines_used = scan(TILE_BLOCKS, row * TILE_BLOCKS, rows)

    @pl.when(slots % 2 == 1)
    def _():
        columns[slots] = columns[slots - 1]

    def pad(at, _):
        rows[at] = TILE_BLOCKS
        return 0

    lax.fori_loop(lines_used, TILE_BLOCKS, pad, 0)

    steps = (slots + 1) // 2

    def tile_copy(step, at):
        block = columns[2 * step + at]
        buffer = step % 2
        return pltpu.make_async_copy(
            inverse.at[:, :, pl.ds(block * BLK, BLK)],
            tiles.at[buffer, :, :, pl.ds(at * BLK, BLK)],
            tile_sems.at[buffer, at],
        )

    for ahead in range(2):

        @pl.when(ahead < steps)
        def _():
            tile_copy(ahead, 0).start()
            tile_copy(ahead, 1).start()

    acc[...] = jnp.zeros_like(acc)
    for copy in copies:
        copy.wait()

    @pl.when(slots % 2 == 1)
    def _():
        panel[slots] = jnp.zeros((BLK // SUB, SUB, W), jnp.float32)

    def prepare(step, _):
        value = panel[pl.ds(2 * step, 2)].reshape(2 * BLK, W)
        high, low = split(value)
        right[step, 0 : 2 * BLK] = high
        right[step, 2 * BLK : 4 * BLK] = low
        right[step, 4 * BLK : 6 * BLK] = high
        return 0

    lax.fori_loop(0, steps, prepare, 0)

    def contract(step, _):
        tile_copy(step, 0).wait()
        tile_copy(step, 1).wait()
        buffer = step % 2

        def narrow(at, _):
            high, low = split(tiles[buffer, rows[at]])
            span = pl.ds(at * BLK, BLK)
            left[span, 0 : 2 * BLK] = high
            left[span, 2 * BLK : 4 * BLK] = high
            left[span, 4 * BLK : 6 * BLK] = low
            return 0

        lax.fori_loop(0, lines_used, narrow, 0)
        for begin, end in CHUNKS:

            @pl.when(lines_used > begin)
            def _():
                part = jnp.dot(
                    left[begin * BLK : end * BLK], right[step], preferred_element_type=jnp.float32
                )
                for at in range(begin, end):
                    acc[rows[at]] += part[(at - begin) * BLK : (at - begin + 1) * BLK]

        @pl.when(step + 2 < steps)
        def _():
            tile_copy(step + 2, 0).start()
            tile_copy(step + 2, 1).start()

        return 0

    lax.fori_loop(0, steps, contract, 0)

    flat = acc.reshape((TILE_BLOCKS + 1) * BLK, W)
    group = TILE_BLOCKS * BLK // (SIDE * CORES)
    out_copies = [pltpu.make_async_copy(flat.at[pl.ds(0, TILE_BLOCKS * BLK)], whole, out_sem.at[8])]
    for at in range(SIDE):
        level = (z + at) % SIDE
        for ref, side in ((mine, core), (theirs, 1 - core)):
            start = pl.multiple_of((level * CORES + side) * group, 32)
            out_copies.append(
                pltpu.make_async_copy(flat.at[pl.ds(start, group)], ref.at[at], out_sem.at[len(out_copies) - 1])
            )
    for copy in out_copies:
        copy.start()
    for copy in out_copies:
        copy.wait()


def tile_product(which, cap, structure, inverse, lines):
    hbm = pl.BlockSpec(memory_space=pl.ANY)
    group = TILE_BLOCKS * BLK // (SIDE * CORES)
    shape = jax.ShapeDtypeStruct((SIDE, group, W), jnp.float32)
    return pl.pallas_call(
        functools.partial(tile_body, which, cap),
        in_specs=[pl.BlockSpec(memory_space=pltpu.SMEM)] + [hbm] * 6,
        out_specs=[hbm] * 3,
        out_shape=[shape, shape, jax.ShapeDtypeStruct((TILE_BLOCKS * BLK, W), jnp.float32)],
        scratch_shapes=[
            pltpu.SMEM((COL_BLOCKS + 2,), jnp.int32),
            pltpu.SMEM((TILE_BLOCKS + 2,), jnp.int32),
            pltpu.VMEM((2, TILE_BLOCKS, BLK, 2 * BLK), jnp.float32),
            pltpu.VMEM((cap, BLK // SUB, SUB, W), jnp.float32),
            pltpu.VMEM((TILE_BLOCKS * BLK, 6 * BLK), jnp.bfloat16),
            pltpu.VMEM((cap // 2, 6 * BLK, W), jnp.bfloat16),
            pltpu.VMEM((TILE_BLOCKS + 1, BLK, W), jnp.float32),
            pltpu.SemaphoreType.DMA((16,)),
            pltpu.SemaphoreType.DMA((2, 2)),
            pltpu.SemaphoreType.DMA((9,)),
        ],
        name="tile_product_%d" % which,
    )(structure, inverse.reshape(TILE_BLOCKS, BLK, COL_BLOCKS * BLK), *lines)


def ring_sum(piece, axis):
    got = [shift(piece(at), axis, at) for at in (1, 2, 3)]
    return piece(0) + got[0] + got[1] + got[2]


def final_sums(terms, mine, theirs, y, x, z, core):
    half = W // CORES

    def columns(side):
        return jnp.concatenate(
            [lax.dynamic_slice_in_dim(term, side * half, half, 1) for term in terms], axis=1
        )

    def take(array, at, dim):
        return lax.dynamic_index_in_dim(array, at % SIDE, dim, keepdims=False)

    chunks = mine + lax.ppermute(theirs, AXES, PARTNER)
    cut = chunks.shape[1] // 2
    value = columns(core) + lax.ppermute(columns(1 - core), AXES, PARTNER)
    cube = value.reshape(SIDE, SIDE, SIDE, SUB, len(terms) * half)
    up = shift(chunks[2, :cut], "zz", 1)
    down = shift(chunks[2, cut:], "zz", -1)
    flat = ring_sum(
        lambda at: jnp.where(core == 0, take(cube, y + at, 0), take(cube, x + at, 1)), "yx"
    )
    flat, up, down = lax.optimization_barrier((flat, up, down))
    above = jnp.concatenate([chunks[1, :cut] + up, chunks[1, cut:]])
    below = jnp.concatenate([chunks[3, :cut], chunks[3, cut:] + down])
    above, below = shift(above, "zz", 1), shift(below, "zz", -1)
    line = ring_sum(lambda at: take(flat, jnp.where(core == 0, x, y) + at, 0), "xy")
    value = ring_sum(lambda at: take(line, z + at, 0), "zz")
    value, above, below = lax.optimization_barrier((value, above, below))
    rows = chunks[0] + above + below
    low, high = value[: SUB // 2], value[SUB // 2 :]
    kept = jnp.where(core == 0, low, high)
    got = lax.ppermute(jnp.where(core == 0, high, low), AXES, PARTNER)
    left, right = jnp.where(core == 0, kept, got), jnp.where(core == 0, got, kept)
    sums = [
        jnp.concatenate([part[:, at * half : (at + 1) * half] for part in (left, right)], axis=1)
        for at in range(len(terms))
    ]
    return rows, sums


def on_device(
    ancestor_inverse, panel_parent, panel_child, coupling, diag_parent, diag_child, structure
):
    row = lax.axis_index("row")
    col = lax.axis_index("col")
    y, x, z, core = row // SIDE, row % SIDE, col // CORES, col % CORES
    caps = CAPS
    tile_rows = panel_parent.shape[0]
    group_rows = tile_rows // (SIDE * CORES)
    own_count = W // (RING * SIDE * CORES)
    own_start = (row * SIDE * CORES + col) * own_count

    panels = jnp.stack([panel_parent, panel_child]).reshape(2, TILE_BLOCKS, BLK // SUB, SUB, W)

    def slices(flip):
        to_y, to_x, _, _ = spread_target(y, x, z, core, flip)
        return lax.dynamic_index_in_dim(panels, to_y * SIDE + to_x, 2, keepdims=False)

    first = lax.ppermute(slices(0), AXES, SPREAD[0])
    second = lax.ppermute(slices(1), AXES, SPREAD[1])
    share = compact(caps, structure, first, second)
    line = gather_line(share, "xy")
    parent_own = jnp.stack([piece[: caps[0]] for piece in line])
    child_own = jnp.stack([piece[caps[0] :] for piece in line])
    parent_near = gather_near(parent_own, "yx")
    parent_near, child_own = lax.optimization_barrier((parent_near, child_own))
    parent_lines = (parent_own, *parent_near, *gather_far(*parent_near, "yx"))
    child_near = gather_near(child_own, "yx")
    child_lines = (child_own, *child_near, *gather_far(*child_near, "yx"))

    flags = lax.dynamic_slice_in_dim(structure[1], row * TILE_BLOCKS, TILE_BLOCKS)
    block_rows = jnp.arange(tile_rows, dtype=jnp.int32)[:, None] // BLK
    hits = (block_rows == jnp.arange(TILE_BLOCKS, dtype=jnp.int32)[None, :]) & (flags[None, :] == 1)
    mask_child = jnp.any(hits, axis=1)[:, None]
    child = jnp.where(mask_child, panel_child, 0)
    mask_group = lax.dynamic_slice_in_dim(mask_child, col * group_rows, group_rows, 0)

    def own_rows(values):
        return lax.dynamic_slice_in_dim(values, own_start, own_count, 0)

    base_top = product(diag_parent, coupling)
    coupling_cols = lax.dynamic_slice_in_dim(coupling, own_start, own_count, 1)
    base_child = own_rows(diag_child) + product_t(coupling_cols, base_top)

    parent_mine, parent_theirs, whole = tile_product(0, caps[0], structure, ancestor_inverse, parent_lines)
    parent_term = product_t(panel_parent, whole)
    cross = product_t(whole, child)
    top_term = product(parent_term, coupling) - cross
    early_child = product_t(coupling, top_term) - product_t(cross, coupling)

    child_mine, child_theirs, whole = tile_product(1, caps[1], structure, ancestor_inverse, child_lines)
    child_term = early_child + product_t(panel_child, whole)
    rows, (parent_sum, top_sum, child_sum) = final_sums(
        [parent_term, top_term, child_term],
        jnp.concatenate([parent_mine, child_mine], axis=2),
        jnp.concatenate([parent_theirs, child_theirs], axis=2),
        y, x, z, core,
    )
    parent_rows = -rows[:, :W]
    child_rows = -(rows[:, W:] + jnp.where(mask_group, product(parent_rows, coupling), 0))
    parent_diag = own_rows(diag_parent) + parent_sum
    child_top = -(own_rows(base_top) + top_sum)
    child_diag = base_child + child_sum
    return parent_rows, parent_diag, child_top, child_rows, child_diag


def solution(mesh):
    return jax.shard_map(
        on_device,
        mesh=mesh,
        in_specs=(P("row", "col"), P("row", None), P("row", None), P(), P(), P(), P()),
        out_specs=(P(AXES, None),) * 5,
        check_vma=False,
    )
```

```python
import functools

import jax
import jax.numpy as jnp
from jax import lax
from jax.experimental import pallas as pl
from jax.experimental.pallas import tpu as pltpu
from jax.sharding import PartitionSpec as P

BLK = 128
SUB = 8
SIDE = 4
CORES = 2
RING = SIDE * SIDE
TILE_BLOCKS = 10
COL_BLOCKS = 20
GROUP = 160
W = 512
AXES = ("row", "col")
SLOTS = 32
CHUNKS = ((0, 6), (6, 10))


def device(y, x, z, core):
    return ((y % SIDE) * SIDE + x % SIDE) * SIDE * CORES + (z % SIDE) * CORES + core


def pairs(target):
    return [
        (device(y, x, z, core), device(*target(y, x, z, core)))
        for y in range(SIDE)
        for x in range(SIDE)
        for z in range(SIDE)
        for core in range(CORES)
    ]


def stepped(axis, by):
    def target(y, x, z, core):
        along = axis[core]
        return y + by * (along == "y"), x + by * (along == "x"), z + by * (along == "z"), core

    return pairs(target)


PARTNER = pairs(lambda y, x, z, core: (y, x, z, 1 - core))


def spread_target(y, x, z, core, flip):
    turn = 2 * core + (x + flip) % 2
    return (y + turn) % SIDE, (x + z + turn) % SIDE, y, x // 2


SPREAD = [
    pairs(lambda y, x, z, core, flip=flip: spread_target(y, x, z, core, flip)) for flip in range(2)
]


def shift(value, axis, by):
    return lax.ppermute(value, AXES, stepped(axis, by))


def product(left, right):
    return jnp.dot(left, right, precision=lax.Precision.HIGH, preferred_element_type=jnp.float32)


def product_t(left, right):
    return lax.dot_general(
        left, right, (((0,), (0,)), ((), ())), precision=lax.Precision.HIGH,
        preferred_element_type=jnp.float32,
    )


def compact_body(turn, structure, first, second, share):
    col = lax.axis_index("col")
    near = (lax.axis_index("row") // SIDE + SIDE - col // CORES) % 2
    slot = -SLOTS * turn[0]
    for which in range(2):

        def step(block, slot):
            flag = structure[which, col * COL_BLOCKS + block]
            part = block // TILE_BLOCKS
            own = block - part * TILE_BLOCKS

            @pl.when((flag == 1) & (slot >= 0) & (slot < SLOTS))
            def _():
                share[slot] = jnp.where(part == near, first[which, own], second[which, own])

            return slot + flag

        slot = lax.fori_loop(0, COL_BLOCKS, step, slot)


def compact(turn, structure, first, second):
    smem = pl.BlockSpec(memory_space=pltpu.SMEM)
    vmem = pl.BlockSpec(memory_space=pltpu.VMEM)
    return pl.pallas_call(
        compact_body,
        in_specs=[smem, smem, vmem, vmem],
        out_specs=vmem,
        out_shape=jax.ShapeDtypeStruct((SLOTS, SUB, W), jnp.float32),
        name="compact",
    )(turn, structure, first, second)


def gather_near(own, axis):
    return shift(own, axis, 1), shift(own, axis, -1)


def gather_far(before, after, axis):
    half = before.shape[0] // 2
    return shift(before[:half], axis, 1), shift(after[half:], axis, -1)


def gather_line(share, axis):
    before, after = gather_near(share, axis)
    far_low, far_high = gather_far(before, after, axis)
    return share, after, jnp.concatenate([far_low, far_high]), before


def split(value):
    high = value.astype(jnp.bfloat16)
    low = (value - high.astype(jnp.float32)).astype(jnp.bfloat16)
    return high, low


def narrow_body(value, high, low):
    high[...], low[...] = split(value[...])


def narrow(inverse):
    spec = pl.BlockSpec((BLK, COL_BLOCKS * BLK), lambda at: (at, 0))
    return pl.pallas_call(
        narrow_body,
        grid=(TILE_BLOCKS,),
        in_specs=[spec],
        out_specs=[spec] * 2,
        out_shape=[jax.ShapeDtypeStruct(inverse.shape, jnp.bfloat16)] * 2,
        cost_estimate=pl.CostEstimate(flops=0, transcendentals=0, bytes_accessed=2 * inverse.size * 4),
        name="narrow",
    )(inverse)


def blank(*shapes):
    hbm = pl.BlockSpec(memory_space=pl.ANY)
    return pl.pallas_call(
        lambda *refs: None,
        out_specs=[hbm] * len(shapes),
        out_shape=[jax.ShapeDtypeStruct(shape, jnp.float32) for shape in shapes],
        name="blank",
    )()


def tile_body(turn, structure, inverse_high, inverse_low, own, before, after, far_low, far_high, whole_old, *refs):
    whole, mine, theirs = refs[2:5]
    blocks, rows, left, panel, right, acc, panel_sem, tile_sems, out_sem = refs[5:]
    row = lax.axis_index("row")
    col = lax.axis_index("col")
    y, x, z, core = row // SIDE, row % SIDE, col // CORES, col % CORES

    pieces = [(own, 0, i, i) for i in range(SIDE)]
    pieces += [(after, 1, i, i) for i in range(SIDE)]
    pieces += [(before, 3, i, i) for i in range(SIDE)]
    pieces += [(far_low, 2, i, i) for i in range(2)]
    pieces += [(far_high, 2, i, i + 2) for i in range(2)]
    copies = []
    for ref, outer, at, inner in pieces:
        sub_y = (y + jnp.where(core == 0, outer, inner)) % SIDE
        sub_x = (x + jnp.where(core == 0, inner, outer)) % SIDE
        copies.append(
            pltpu.make_async_copy(
                ref.at[at],
                panel.at[pl.ds(0, SLOTS), sub_y * SIDE + sub_x],
                panel_sem.at[len(copies)],
            )
        )
    for copy in copies:
        copy.start()

    def scan_columns(which, count):
        def step(block, slot):
            flag = structure[which, col * COL_BLOCKS + block]

            @pl.when(flag == 1)
            def _():
                blocks[slot] = block

            return slot + flag

        return lax.fori_loop(0, COL_BLOCKS, step, count)

    def scan_rows(which):
        def step(block, slot):
            flag = structure[which, row * TILE_BLOCKS + block]

            @pl.when(flag == 1)
            def _():
                rows[which, slot] = block

            return slot + flag

        used = lax.fori_loop(0, TILE_BLOCKS, step, 0)

        def pad(at, _):
            rows[which, at] = TILE_BLOCKS
            return 0

        lax.fori_loop(used, TILE_BLOCKS, pad, 0)
        return used

    parents = scan_columns(0, 0)
    both = scan_columns(1, parents)
    parent_lines, child_lines = scan_rows(0), scan_rows(1)
    first = SLOTS * turn[0]
    last = first + SLOTS
    parent_begin, parent_end = jnp.minimum(first, parents), jnp.minimum(last, parents)
    child_begin = jnp.clip(first, parents, both)
    child_end = jnp.clip(last, parents, both)
    parent_steps = (parent_end - parent_begin + 1) // 2
    steps = parent_steps + (child_end - child_begin + 1) // 2

    def slots_of(step):
        is_child = step >= parent_steps
        slot = jnp.where(is_child, child_begin + 2 * (step - parent_steps), parent_begin + 2 * step)
        return slot, jnp.where(is_child, child_end, parent_end)

    def tile_copies(step):
        slot, end = slots_of(step)
        buffer = step % 2
        copies = []
        for at in range(2):
            block = blocks[jnp.minimum(slot + at, end - 1)]
            for part, ref in enumerate((inverse_high, inverse_high, inverse_low)):
                copies.append(
                    pltpu.make_async_copy(
                        ref.at[:, :, pl.ds(pl.multiple_of(block * BLK, BLK), BLK)],
                        left.at[buffer, :, :, pl.ds((2 * part + at) * BLK, BLK)],
                        tile_sems.at[buffer, 3 * at + part],
                    )
                )
        return copies

    for ahead in range(2):

        @pl.when(ahead < steps)
        def _():
            for copy in tile_copies(ahead):
                copy.start()

    @pl.when(turn[0] == 0)
    def _():
        acc[...] = jnp.zeros_like(acc)

    @pl.when(turn[0] > 0)
    def _():
        old = pltpu.make_async_copy(whole_old, acc.at[:, pl.ds(0, TILE_BLOCKS)], out_sem.at[0])
        old.start()
        old.wait()

    panel[SLOTS] = jnp.zeros((BLK // SUB, SUB, W), jnp.float32)
    for copy in copies:
        copy.wait()

    def contract(which, lines, step):
        for copy in tile_copies(step):
            copy.wait()
        buffer = step % 2
        slot, end = slots_of(step)
        for at in range(2):
            here = jnp.where(slot + at < end, slot + at - first, SLOTS)
            high, low = split(panel[here].reshape(BLK, W))
            right[pl.ds(at * BLK, BLK)] = high
            right[pl.ds((2 + at) * BLK, BLK)] = low
            right[pl.ds((4 + at) * BLK, BLK)] = high

        for begin, stop in CHUNKS:

            @pl.when(lines > begin)
            def _():
                picked = [rows[which, at] for at in range(begin, stop)]
                value = jnp.concatenate(
                    [left[buffer, jnp.minimum(at, TILE_BLOCKS - 1)] for at in picked], axis=0
                )
                part = jnp.dot(value, right[...], preferred_element_type=jnp.float32)
                for index, at in enumerate(picked):
                    acc[which, at] += part[index * BLK : (index + 1) * BLK]

        @pl.when(step + 2 < steps)
        def _():
            for copy in tile_copies(step + 2):
                copy.start()

    flat = acc.reshape(2, (TILE_BLOCKS + 1) * BLK, W)
    out_copies = []
    for which in range(2):
        made = [(acc.at[which, pl.ds(0, TILE_BLOCKS)], whole.at[which])]
        for at in range(SIDE):
            level = (z + at) % SIDE
            for ref, side in ((mine, core), (theirs, 1 - core)):
                start = pl.multiple_of((level * CORES + side) * GROUP, 32)
                made.append((flat.at[which, pl.ds(start, GROUP)], ref.at[at, :, pl.ds(which * W, W)]))
        out_copies.append(
            [
                pltpu.make_async_copy(source, to, out_sem.at[len(made) * which + at])
                for at, (source, to) in enumerate(made)
            ]
        )

    def parent_step(step, _):
        contract(0, parent_lines, step)
        return 0

    def child_step(step, _):
        contract(1, child_lines, step)
        return 0

    lax.fori_loop(0, parent_steps, parent_step, 0)
    for copy in out_copies[0]:
        copy.start()
    lax.fori_loop(parent_steps, steps, child_step, 0)
    for copy in out_copies[1]:
        copy.start()
    for copy in out_copies[0] + out_copies[1]:
        copy.wait()


def tile_products(turn, structure, inverse_parts, lines, old):
    hbm = pl.BlockSpec(memory_space=pl.ANY)
    smem = pl.BlockSpec(memory_space=pltpu.SMEM)
    return pl.pallas_call(
        tile_body,
        in_specs=[smem, smem] + [hbm] * 10,
        out_specs=[hbm] * 3,
        out_shape=[jax.ShapeDtypeStruct(array.shape, array.dtype) for array in old],
        input_output_aliases={9: 0, 10: 1, 11: 2},
        scratch_shapes=[
            pltpu.SMEM((2 * COL_BLOCKS,), jnp.int32),
            pltpu.SMEM((2, TILE_BLOCKS), jnp.int32),
            pltpu.VMEM((2, TILE_BLOCKS, BLK, 6 * BLK), jnp.bfloat16),
            pltpu.VMEM((SLOTS + 1, BLK // SUB, SUB, W), jnp.float32),
            pltpu.VMEM((6 * BLK, W), jnp.bfloat16),
            pltpu.VMEM((2, TILE_BLOCKS + 1, BLK, W), jnp.float32),
            pltpu.SemaphoreType.DMA((16,)),
            pltpu.SemaphoreType.DMA((2, 6)),
            pltpu.SemaphoreType.DMA((18,)),
        ],
        name="tile_products",
    )(
        turn,
        structure,
        *(part.reshape(TILE_BLOCKS, BLK, COL_BLOCKS * BLK) for part in inverse_parts),
        *lines,
        *old,
    )


def ring_sum(piece, axis):
    got = [shift(piece(at), axis, at) for at in (1, 2, 3)]
    return piece(0) + got[0] + got[1] + got[2]


def final_sums(terms, chunks, up, down, y, x, z, core):
    half = W // CORES

    def columns(side):
        return jnp.concatenate(
            [lax.dynamic_slice_in_dim(term, side * half, half, 1) for term in terms], axis=1
        )

    def take(array, at, dim):
        return lax.dynamic_index_in_dim(array, at % SIDE, dim, keepdims=False)

    cut = chunks.shape[1] // 2
    value = columns(core) + lax.ppermute(columns(1 - core), AXES, PARTNER)
    cube = value.reshape(SIDE, SIDE, SIDE, SUB, len(terms) * half)
    above = jnp.concatenate([chunks[1, :cut] + up, chunks[1, cut:]])
    below = jnp.concatenate([chunks[3, :cut], chunks[3, cut:] + down])
    above, below = shift(above, "zz", 1), shift(below, "zz", -1)
    flat = ring_sum(
        lambda at: jnp.where(core == 0, take(cube, y + at, 0), take(cube, x + at, 1)), "yx"
    )
    line = ring_sum(lambda at: take(flat, jnp.where(core == 0, x, y) + at, 0), "xy")
    value = ring_sum(lambda at: take(line, z + at, 0), "zz")
    value, above, below = lax.optimization_barrier((value, above, below))
    rows = chunks[0] + above + below
    low, high = value[: SUB // 2], value[SUB // 2 :]
    kept = jnp.where(core == 0, low, high)
    got = lax.ppermute(jnp.where(core == 0, high, low), AXES, PARTNER)
    left, right = jnp.where(core == 0, kept, got), jnp.where(core == 0, got, kept)
    sums = [
        jnp.concatenate([part[:, at * half : (at + 1) * half] for part in (left, right)], axis=1)
        for at in range(len(terms))
    ]
    return rows, sums


def on_device(
    ancestor_inverse, panel_parent, panel_child, coupling, diag_parent, diag_child, structure
):
    row = lax.axis_index("row")
    col = lax.axis_index("col")
    y, x, z, core = row // SIDE, row % SIDE, col // CORES, col % CORES
    tile_rows = panel_parent.shape[0]
    group_rows = tile_rows // (SIDE * CORES)
    own_count = W // (RING * SIDE * CORES)
    own_start = (row * SIDE * CORES + col) * own_count

    panels = jnp.stack([panel_parent, panel_child]).reshape(2, TILE_BLOCKS, BLK // SUB, SUB, W)

    def slices(flip):
        to_y, to_x, _, _ = spread_target(y, x, z, core, flip)
        return lax.dynamic_index_in_dim(panels, to_y * SIDE + to_x, 2, keepdims=False)

    first = lax.ppermute(slices(0), AXES, SPREAD[0])
    second = lax.ppermute(slices(1), AXES, SPREAD[1])
    counts = structure.reshape(2, SIDE * CORES, COL_BLOCKS).sum(axis=(0, 2))
    turns = (jnp.max(counts) + SLOTS - 1) // SLOTS

    def one_turn(at, old):
        turn = jnp.reshape(at, (1,))
        share = compact(turn, structure, first, second)
        line = jnp.stack(gather_line(share, "xy"))
        near = gather_near(line, "yx")
        near, parts = lax.optimization_barrier((near, narrow(ancestor_inverse)))
        lines = (line, *near, *gather_far(*near, "yx"))
        return tuple(tile_products(turn, structure, parts, lines, old))

    start = tuple(
        blank((2, TILE_BLOCKS, BLK, W), (SIDE, GROUP, 2 * W), (SIDE, GROUP, 2 * W))
    )
    whole, mine, theirs = lax.fori_loop(0, turns, one_turn, start)
    parent_whole = whole[0].reshape(tile_rows, W)
    child_whole = whole[1].reshape(tile_rows, W)

    flags = lax.dynamic_slice_in_dim(structure[1], row * TILE_BLOCKS, TILE_BLOCKS)
    block_rows = jnp.arange(tile_rows, dtype=jnp.int32)[:, None] // BLK
    hits = (block_rows == jnp.arange(TILE_BLOCKS, dtype=jnp.int32)[None, :]) & (flags[None, :] == 1)
    mask_child = jnp.any(hits, axis=1)[:, None]
    child = jnp.where(mask_child, panel_child, 0)
    mask_group = lax.dynamic_slice_in_dim(mask_child, col * group_rows, group_rows, 0)

    def own_rows(values):
        return lax.dynamic_slice_in_dim(values, own_start, own_count, 0)

    base_top = product(diag_parent, coupling)
    coupling_cols = lax.dynamic_slice_in_dim(coupling, own_start, own_count, 1)
    base_child = own_rows(diag_child) + product_t(coupling_cols, base_top)

    chunks = mine + lax.ppermute(theirs, AXES, PARTNER)
    cut = GROUP // 2
    up, down = shift(chunks[2, :cut], "zz", 1), shift(chunks[2, cut:], "zz", -1)
    parent_term = product_t(panel_parent, parent_whole)
    cross = product_t(parent_whole, child)
    child_whole, up, down = lax.optimization_barrier((child_whole, up, down))
    top_term = product(parent_term, coupling) - cross
    child_term = (
        product_t(coupling, top_term) - product_t(cross, coupling) + product_t(panel_child, child_whole)
    )
    rows, (parent_sum, top_sum, child_sum) = final_sums(
        [parent_term, top_term, child_term], chunks, up, down, y, x, z, core
    )
    parent_rows = -rows[:, :W]
    child_rows = -(rows[:, W:] + jnp.where(mask_group, product(parent_rows, coupling), 0))
    parent_diag = own_rows(diag_parent) + parent_sum
    child_top = -(own_rows(base_top) + top_sum)
    child_diag = base_child + child_sum
    return parent_rows, parent_diag, child_top, child_rows, child_diag


def solution(mesh):
    return jax.shard_map(
        on_device,
        mesh=mesh,
        in_specs=(P("row", "col"), P("row", None), P("row", None), P(), P(), P(), P()),
        out_specs=(P(AXES, None),) * 5,
        check_vma=False,
    )
```

```python
import jax
import jax.numpy as jnp
from jax import lax
from jax.experimental import pallas as pl
from jax.experimental.pallas import tpu as pltpu
from jax.sharding import PartitionSpec as P


BLK = 128
SUB = 8
SIDE = 4
CORES = 2
RING = SIDE * SIDE
TILE_BLOCKS = 10
COL_BLOCKS = 20
GROUP = 160
W = 512
AXES = ("row", "col")
SLOTS = 32
CHUNKS = ((0, 6), (6, 10))


def device(y, x, z, core):
    return ((y % SIDE) * SIDE + x % SIDE) * SIDE * CORES + (z % SIDE) * CORES + core


def pairs(target):
    return [
        (device(y, x, z, core), device(*target(y, x, z, core)))
        for y in range(SIDE)
        for x in range(SIDE)
        for z in range(SIDE)
        for core in range(CORES)
    ]


def stepped(axis, by):
    def target(y, x, z, core):
        along = axis[core]
        return y + by * (along == "y"), x + by * (along == "x"), z + by * (along == "z"), core

    return pairs(target)


PARTNER = pairs(lambda y, x, z, core: (y, x, z, 1 - core))


def spread_target(y, x, z, core, flip):
    turn = 2 * core + (x + flip) % 2
    return (y + turn) % SIDE, (x + z + turn) % SIDE, y, x // 2


SPREAD = [
    pairs(lambda y, x, z, core, flip=flip: spread_target(y, x, z, core, flip)) for flip in range(2)
]


def shift(value, axis, by):
    return lax.ppermute(value, AXES, stepped(axis, by))


def product(left, right):
    return jnp.dot(left, right, precision=lax.Precision.HIGH, preferred_element_type=jnp.float32)


def product_t(left, right):
    return lax.dot_general(
        left, right, (((0,), (0,)), ((), ())), precision=lax.Precision.HIGH,
        preferred_element_type=jnp.float32,
    )


def compact_body(turn, structure, first, second, share):
    col = lax.axis_index("col")
    near = (lax.axis_index("row") // SIDE + SIDE - col // CORES) % 2
    slot = -SLOTS * turn[0]
    for which in range(2):

        def step(block, slot):
            flag = structure[which, col * COL_BLOCKS + block]
            part = block // TILE_BLOCKS
            own = block - part * TILE_BLOCKS

            @pl.when((flag == 1) & (slot >= 0) & (slot < SLOTS))
            def _():
                share[slot] = jnp.where(part == near, first[which, own], second[which, own])

            return slot + flag

        slot = lax.fori_loop(0, COL_BLOCKS, step, slot)


def compact(turn, structure, first, second):
    smem = pl.BlockSpec(memory_space=pltpu.SMEM)
    vmem = pl.BlockSpec(memory_space=pltpu.VMEM)
    return pl.pallas_call(
        compact_body,
        in_specs=[smem, smem, vmem, vmem],
        out_specs=vmem,
        out_shape=jax.ShapeDtypeStruct((SLOTS, SUB, W), jnp.float32),
        name="compact",
    )(turn, structure, first, second)


def gather_near(own, axis):
    return shift(own, axis, 1), shift(own, axis, -1)


def gather_far(before, after, axis):
    half = before.shape[0] // 2
    return shift(before[:half], axis, 1), shift(after[half:], axis, -1)


def gather_line(share, axis):
    before, after = gather_near(share, axis)
    far_low, far_high = gather_far(before, after, axis)
    return share, after, jnp.concatenate([far_low, far_high]), before


def split(value):
    high = value.astype(jnp.bfloat16)
    low = (value - high.astype(jnp.float32)).astype(jnp.bfloat16)
    return high, low


def narrow_body(value, parts):
    for block in range(COL_BLOCKS):
        high, low = split(value[:, block * BLK : (block + 1) * BLK])
        parts[block, :, :BLK] = high
        parts[block, :, BLK:] = low


def narrow(inverse):
    rows, cols = inverse.shape
    return pl.pallas_call(
        narrow_body,
        grid=(TILE_BLOCKS,),
        in_specs=[pl.BlockSpec((BLK, cols), lambda at: (at, 0))],
        out_specs=pl.BlockSpec((COL_BLOCKS, BLK, 2 * BLK), lambda at: (0, at, 0)),
        out_shape=jax.ShapeDtypeStruct((COL_BLOCKS, rows, 2 * BLK), jnp.bfloat16),
        cost_estimate=pl.CostEstimate(flops=0, transcendentals=0, bytes_accessed=2 * inverse.size * 4),
        name="narrow",
    )(inverse)


def blank(*shapes):
    hbm = pl.BlockSpec(memory_space=pl.ANY)
    return pl.pallas_call(
        lambda *refs: None,
        out_specs=[hbm] * len(shapes),
        out_shape=[jax.ShapeDtypeStruct(shape, jnp.float32) for shape in shapes],
        name="blank",
    )()


def tile_body(turn, structure, parts, own, before, after, far_low, far_high, whole_old, *refs):
    whole, mine, theirs = refs[2:5]
    blocks, rows, left, panel, right, acc, panel_sem, tile_sems, out_sem = refs[5:]
    row = lax.axis_index("row")
    col = lax.axis_index("col")
    y, x, z, core = row // SIDE, row % SIDE, col // CORES, col % CORES

    pieces = [(own, 0, i, i) for i in range(SIDE)]
    pieces += [(after, 1, i, i) for i in range(SIDE)]
    pieces += [(before, 3, i, i) for i in range(SIDE)]
    pieces += [(far_low, 2, i, i) for i in range(2)]
    pieces += [(far_high, 2, i, i + 2) for i in range(2)]
    copies = []
    for ref, outer, at, inner in pieces:
        sub_y = (y + jnp.where(core == 0, outer, inner)) % SIDE
        sub_x = (x + jnp.where(core == 0, inner, outer)) % SIDE
        copies.append(
            pltpu.make_async_copy(
                ref.at[at],
                panel.at[pl.ds(0, SLOTS), sub_y * SIDE + sub_x],
                panel_sem.at[len(copies)],
            )
        )
    for copy in copies:
        copy.start()

    def scan_columns(which, count):
        def step(block, slot):
            flag = structure[which, col * COL_BLOCKS + block]

            @pl.when(flag == 1)
            def _():
                blocks[slot] = block

            return slot + flag

        return lax.fori_loop(0, COL_BLOCKS, step, count)

    def scan_rows(which):
        def step(block, slot):
            flag = structure[which, row * TILE_BLOCKS + block]

            @pl.when(flag == 1)
            def _():
                rows[which, slot] = block

            return slot + flag

        used = lax.fori_loop(0, TILE_BLOCKS, step, 0)

        def pad(at, _):
            rows[which, at] = TILE_BLOCKS
            return 0

        lax.fori_loop(used, TILE_BLOCKS, pad, 0)
        return used

    parents = scan_columns(0, 0)
    both = scan_columns(1, parents)
    parent_lines, child_lines = scan_rows(0), scan_rows(1)
    first = SLOTS * turn[0]
    last = first + SLOTS
    parent_begin, parent_end = jnp.minimum(first, parents), jnp.minimum(last, parents)
    child_begin = jnp.clip(first, parents, both)
    child_end = jnp.clip(last, parents, both)
    parent_steps = (parent_end - parent_begin + 1) // 2
    steps = parent_steps + (child_end - child_begin + 1) // 2

    def slots_of(step):
        is_child = step >= parent_steps
        slot = jnp.where(is_child, child_begin + 2 * (step - parent_steps), parent_begin + 2 * step)
        return slot, jnp.where(is_child, child_end, parent_end)

    def tile_copies(step):
        slot, end = slots_of(step)
        buffer = step % 2
        copies = []
        for at in range(2):
            block = blocks[jnp.minimum(slot + at, end - 1)]
            copies.append(
                pltpu.make_async_copy(
                    parts.at[block],
                    left.at[buffer, :, :, pl.ds(2 * at * BLK, 2 * BLK)],
                    tile_sems.at[buffer, at],
                )
            )
        return copies

    for ahead in range(2):

        @pl.when(ahead < steps)
        def _():
            for copy in tile_copies(ahead):
                copy.start()

    @pl.when(turn[0] == 0)
    def _():
        acc[...] = jnp.zeros_like(acc)

    @pl.when(turn[0] > 0)
    def _():
        old = pltpu.make_async_copy(whole_old, acc.at[:, pl.ds(0, TILE_BLOCKS)], out_sem.at[0])
        old.start()
        old.wait()

    panel[SLOTS] = jnp.zeros((BLK // SUB, SUB, W), jnp.float32)
    for copy in copies:
        copy.wait()

    def contract(which, lines, step):
        for copy in tile_copies(step):
            copy.wait()
        buffer = step % 2
        slot, end = slots_of(step)
        for at in range(2):
            here = jnp.where(slot + at < end, slot + at - first, SLOTS)
            high, low = split(panel[here].reshape(BLK, W))
            right[pl.ds(2 * at * BLK, BLK)] = high
            right[pl.ds((2 * at + 1) * BLK, BLK)] = high
            right[pl.ds((4 + at) * BLK, BLK)] = low

        for begin, stop in CHUNKS:

            @pl.when(lines > begin)
            def _():
                picked = [rows[which, at] for at in range(begin, stop)]
                value = jnp.concatenate(
                    [left[buffer, jnp.minimum(at, TILE_BLOCKS - 1)] for at in picked], axis=0
                )
                value = jnp.concatenate(
                    [value, value[:, :BLK], value[:, 2 * BLK : 3 * BLK]], axis=1
                )
                part = jnp.dot(value, right[...], preferred_element_type=jnp.float32)
                for index, at in enumerate(picked):
                    acc[which, at] += part[index * BLK : (index + 1) * BLK]

        @pl.when(step + 2 < steps)
        def _():
            for copy in tile_copies(step + 2):
                copy.start()

    flat = acc.reshape(2, (TILE_BLOCKS + 1) * BLK, W)
    out_copies = []
    for which in range(2):
        made = [(acc.at[which, pl.ds(0, TILE_BLOCKS)], whole.at[which])]
        for at in range(SIDE):
            level = (z + at) % SIDE
            for ref, side in ((mine, core), (theirs, 1 - core)):
                start = pl.multiple_of((level * CORES + side) * GROUP, 32)
                made.append((flat.at[which, pl.ds(start, GROUP)], ref.at[at, :, pl.ds(which * W, W)]))
        out_copies.append(
            [
                pltpu.make_async_copy(source, to, out_sem.at[len(made) * which + at])
                for at, (source, to) in enumerate(made)
            ]
        )

    def parent_step(step, _):
        contract(0, parent_lines, step)
        return 0

    def child_step(step, _):
        contract(1, child_lines, step)
        return 0

    lax.fori_loop(0, parent_steps, parent_step, 0)
    for copy in out_copies[0]:
        copy.start()
    lax.fori_loop(parent_steps, steps, child_step, 0)
    for copy in out_copies[1]:
        copy.start()
    for copy in out_copies[0] + out_copies[1]:
        copy.wait()


def tile_products(turn, structure, parts, lines, old):
    hbm = pl.BlockSpec(memory_space=pl.ANY)
    smem = pl.BlockSpec(memory_space=pltpu.SMEM)
    return pl.pallas_call(
        tile_body,
        in_specs=[smem, smem] + [hbm] * 9,
        out_specs=[hbm] * 3,
        out_shape=[jax.ShapeDtypeStruct(array.shape, array.dtype) for array in old],
        input_output_aliases={8: 0, 9: 1, 10: 2},
        scratch_shapes=[
            pltpu.SMEM((2 * COL_BLOCKS,), jnp.int32),
            pltpu.SMEM((2, TILE_BLOCKS), jnp.int32),
            pltpu.VMEM((2, TILE_BLOCKS, BLK, 4 * BLK), jnp.bfloat16),
            pltpu.VMEM((SLOTS + 1, BLK // SUB, SUB, W), jnp.float32),
            pltpu.VMEM((6 * BLK, W), jnp.bfloat16),
            pltpu.VMEM((2, TILE_BLOCKS + 1, BLK, W), jnp.float32),
            pltpu.SemaphoreType.DMA((16,)),
            pltpu.SemaphoreType.DMA((2, 2)),
            pltpu.SemaphoreType.DMA((18,)),
        ],
        name="tile_products",
    )(
        turn,
        structure,
        parts.reshape(COL_BLOCKS, TILE_BLOCKS, BLK, 2 * BLK),
        *lines,
        *old,
    )


def ring_sum(piece, axis):
    got = []
    for at in (1, 2, 3):
        got.append(shift(piece(at), axis, at))
    return piece(0) + got[0] + got[1] + got[2]


def final_sums(terms, chunks, up, down, y, x, z, core):
    half = W // CORES

    def columns(side):
        return jnp.concatenate(
            [lax.dynamic_slice_in_dim(term, side * half, half, 1) for term in terms], axis=1
        )

    def take(array, at, dim):
        return lax.dynamic_index_in_dim(array, at % SIDE, dim, keepdims=False)

    cut = chunks.shape[1] // 2
    got = lax.ppermute(columns(1 - core), AXES, PARTNER)
    value = columns(core) + got
    cube = value.reshape(SIDE, SIDE, SIDE, SUB, len(terms) * half)
    above = jnp.concatenate([chunks[1, :cut] + up, chunks[1, cut:]])
    below = jnp.concatenate([chunks[3, :cut], chunks[3, cut:] + down])
    above = shift(above, "zz", 1)
    below = shift(below, "zz", -1)
    flat = ring_sum(
        lambda at: jnp.where(core == 0, take(cube, y + at, 0), take(cube, x + at, 1)), "yx"
    )
    line = ring_sum(lambda at: take(flat, jnp.where(core == 0, x, y) + at, 0), "xy")
    value = ring_sum(lambda at: take(line, z + at, 0), "zz")
    value, above, below = lax.optimization_barrier((value, above, below))
    rows = chunks[0] + above + below
    low, high = value[: SUB // 2], value[SUB // 2 :]
    kept = jnp.where(core == 0, low, high)
    got = lax.ppermute(jnp.where(core == 0, high, low), AXES, PARTNER)
    left, right = jnp.where(core == 0, kept, got), jnp.where(core == 0, got, kept)
    sums = [
        jnp.concatenate([part[:, at * half : (at + 1) * half] for part in (left, right)], axis=1)
        for at in range(len(terms))
    ]
    return rows, sums


def invert(
    ancestor_inverse, panel_parent, panel_child, coupling, diag_parent, diag_child, structure
):
    row = lax.axis_index("row")
    col = lax.axis_index("col")
    y, x, z, core = row // SIDE, row % SIDE, col // CORES, col % CORES
    tile_rows = panel_parent.shape[0]
    group_rows = tile_rows // (SIDE * CORES)
    own_count = W // (RING * SIDE * CORES)
    own_start = (row * SIDE * CORES + col) * own_count

    panels = jnp.stack([panel_parent, panel_child]).reshape(2, TILE_BLOCKS, BLK // SUB, SUB, W)

    def slices(flip):
        to_y, to_x, _, _ = spread_target(y, x, z, core, flip)
        return lax.dynamic_index_in_dim(panels, to_y * SIDE + to_x, 2, keepdims=False)

    first = lax.ppermute(slices(0), AXES, SPREAD[0])
    second = lax.ppermute(slices(1), AXES, SPREAD[1])
    counts = structure.reshape(2, SIDE * CORES, COL_BLOCKS).sum(axis=(0, 2))
    turns = (jnp.max(counts) + SLOTS - 1) // SLOTS

    def one_turn(at, old):
        turn = jnp.reshape(at, (1,))
        share = compact(turn, structure, first, second)
        line = jnp.stack(gather_line(share, "xy"))
        near = gather_near(line, "yx")
        near, parts = lax.optimization_barrier((near, narrow(ancestor_inverse)))
        lines = (line, *near, *gather_far(*near, "yx"))
        return tuple(tile_products(turn, structure, parts, lines, old))

    start = tuple(
        blank((2, TILE_BLOCKS, BLK, W), (SIDE, GROUP, 2 * W), (SIDE, GROUP, 2 * W))
    )
    whole, mine, theirs = lax.fori_loop(0, turns, one_turn, start)
    parent_whole = whole[0].reshape(tile_rows, W)
    child_whole = whole[1].reshape(tile_rows, W)

    flags = lax.dynamic_slice_in_dim(structure[1], row * TILE_BLOCKS, TILE_BLOCKS)
    block_rows = jnp.arange(tile_rows, dtype=jnp.int32)[:, None] // BLK
    hits = (block_rows == jnp.arange(TILE_BLOCKS, dtype=jnp.int32)[None, :]) & (flags[None, :] == 1)
    mask_child = jnp.any(hits, axis=1)[:, None]
    child = jnp.where(mask_child, panel_child, 0)
    mask_group = lax.dynamic_slice_in_dim(mask_child, col * group_rows, group_rows, 0)

    def own_rows(values):
        return lax.dynamic_slice_in_dim(values, own_start, own_count, 0)

    base_top = product(diag_parent, coupling)
    coupling_cols = lax.dynamic_slice_in_dim(coupling, own_start, own_count, 1)
    base_child = own_rows(diag_child) + product_t(coupling_cols, base_top)

    chunks = mine + lax.ppermute(theirs, AXES, PARTNER)
    cut = GROUP // 2
    up = shift(chunks[2, :cut], "zz", 1)
    down = shift(chunks[2, cut:], "zz", -1)
    parent_term = product_t(panel_parent, parent_whole)
    cross = product_t(parent_whole, child)
    top_term = product(parent_term, coupling) - cross
    child_term = (
        product_t(coupling, top_term) - product_t(cross, coupling) + product_t(panel_child, child_whole)
    )
    rows, (parent_sum, top_sum, child_sum) = final_sums(
        [parent_term, top_term, child_term], chunks, up, down, y, x, z, core
    )
    parent_rows = -rows[:, :W]
    child_rows = -(rows[:, W:] + jnp.where(mask_group, product(parent_rows, coupling), 0))
    parent_diag = own_rows(diag_parent) + parent_sum
    child_top = -(own_rows(base_top) + top_sum)
    child_diag = base_child + child_sum
    return parent_rows, parent_diag, child_top, child_rows, child_diag


def solution(mesh):
    return jax.shard_map(
        invert,
        mesh=mesh,
        in_specs=(P("row", "col"), P("row", None), P("row", None), P(), P(), P(), P()),
        out_specs=(P(AXES, None),) * 5,
        check_vma=False,
    )
```

```python
import itertools

import jax
import jax.numpy as jnp
from jax import lax
from jax.experimental import pallas as pl
from jax.experimental.pallas import tpu as pltpu
from jax.sharding import PartitionSpec as P


BLK = 128
SUB = 8
SIDE = 4
CORES = 2
RING = SIDE * SIDE
TILE_BLOCKS = 10
COL_BLOCKS = 20
GROUP = 160
W = 512
AXES = ("row", "col")
SLOTS = 32
FEW = 6
EARLY = SLOTS // 2


def device(y, x, z, core):
    return ((y % SIDE) * SIDE + x % SIDE) * SIDE * CORES + (z % SIDE) * CORES + core


def pairs(target):
    return [
        (device(y, x, z, core), device(*target(y, x, z, core)))
        for y in range(SIDE)
        for x in range(SIDE)
        for z in range(SIDE)
        for core in range(CORES)
    ]


def stepped(axis, by):
    def target(y, x, z, core):
        along = axis[core]
        return y + by * (along == "y"), x + by * (along == "x"), z + by * (along == "z"), core

    return pairs(target)


PARTNER = pairs(lambda y, x, z, core: (y, x, z, 1 - core))


def spread_target(y, x, z, core, flip):
    turn = 2 * core + (x + flip) % 2
    return (y + turn) % SIDE, (x + z + turn) % SIDE, y, x // 2


SPREAD = [
    pairs(lambda y, x, z, core, flip=flip: spread_target(y, x, z, core, flip)) for flip in range(2)
]


def shift(value, axis, by):
    return lax.ppermute(value, AXES, stepped(axis, by))


def product(left, right):
    return jnp.dot(left, right, precision=lax.Precision.HIGH, preferred_element_type=jnp.float32)


def product_t(left, right):
    return lax.dot_general(
        left, right, (((0,), (0,)), ((), ())), precision=lax.Precision.HIGH,
        preferred_element_type=jnp.float32,
    )


def compact_body(turn, structure, first, second, share):
    col = lax.axis_index("col")
    near = (lax.axis_index("row") // SIDE + SIDE - col // CORES) % 2
    slot = -SLOTS * turn[0]
    for which in range(2):

        def step(block, slot):
            flag = structure[which, col * COL_BLOCKS + block]
            part = block // TILE_BLOCKS
            own = block - part * TILE_BLOCKS

            @pl.when((flag == 1) & (slot >= 0) & (slot < SLOTS))
            def _():
                share[slot] = jnp.where(part == near, first[which, own], second[which, own])

            return slot + flag

        slot = lax.fori_loop(0, COL_BLOCKS, step, slot)


def compact(turn, structure, first, second):
    smem = pl.BlockSpec(memory_space=pltpu.SMEM)
    vmem = pl.BlockSpec(memory_space=pltpu.VMEM)
    return pl.pallas_call(
        compact_body,
        in_specs=[smem, smem, vmem, vmem],
        out_specs=vmem,
        out_shape=jax.ShapeDtypeStruct((SLOTS, SUB, W), jnp.float32),
        name="compact",
    )(turn, structure, first, second)


def gather_near(own, axis):
    return shift(own, axis, 1), shift(own, axis, -1)


def gather_far(before, after, axis):
    half = before.shape[0] // 2
    return shift(before[:half], axis, 1), shift(after[half:], axis, -1)


def gather_line(share, axis):
    before, after = gather_near(share, axis)
    far_low, far_high = gather_far(before, after, axis)
    return share, after, jnp.concatenate([far_low, far_high]), before


def split(value):
    high = value.astype(jnp.bfloat16)
    low = (value - high.astype(jnp.float32)).astype(jnp.bfloat16)
    return high, low


def narrow_body(value, parts):
    for block in range(COL_BLOCKS):
        high, low = split(value[:, block * BLK : (block + 1) * BLK])
        parts[block, :, :BLK] = high
        parts[block, :, BLK:] = low


def narrow(inverse):
    rows, cols = inverse.shape
    return pl.pallas_call(
        narrow_body,
        grid=(TILE_BLOCKS,),
        in_specs=[pl.BlockSpec((BLK, cols), lambda at: (at, 0))],
        out_specs=pl.BlockSpec((COL_BLOCKS, BLK, 2 * BLK), lambda at: (0, at, 0)),
        out_shape=jax.ShapeDtypeStruct((COL_BLOCKS, rows, 2 * BLK), jnp.bfloat16),
        cost_estimate=pl.CostEstimate(flops=0, transcendentals=0, bytes_accessed=2 * inverse.size * 4),
        name="narrow",
    )(inverse)


def blank(*shapes):
    hbm = pl.BlockSpec(memory_space=pl.ANY)
    return pl.pallas_call(
        lambda *refs: None,
        out_specs=[hbm] * len(shapes),
        out_shape=[jax.ShapeDtypeStruct(shape, jnp.float32) for shape in shapes],
        name="blank",
    )()


def tile_body(turn, structure, parts, own, before, after, far_low, far_high, whole_old, *refs):
    whole, mine, theirs = refs[2:5]
    blocks, rows, left, panel, right, acc, panel_sem, tile_sems, out_sem = refs[5:]
    row = lax.axis_index("row")
    col = lax.axis_index("col")
    y, x, z, core = row // SIDE, row % SIDE, col // CORES, col % CORES

    pieces = [(own, 0, i, i) for i in range(SIDE)]
    pieces += [(after, 1, i, i) for i in range(SIDE)]
    pieces += [(before, 3, i, i) for i in range(SIDE)]
    pieces += [(far_low, 2, i, i) for i in range(2)]
    pieces += [(far_high, 2, i, i + 2) for i in range(2)]
    copies = []
    for half, (ref, outer, at, inner) in itertools.product(range(2), pieces):
        span = pl.ds(half * EARLY, EARLY)
        sub_y = (y + jnp.where(core == 0, outer, inner)) % SIDE
        sub_x = (x + jnp.where(core == 0, inner, outer)) % SIDE
        copies.append(
            pltpu.make_async_copy(
                ref.at[at, span],
                panel.at[span, sub_y * SIDE + sub_x],
                panel_sem.at[len(copies)],
            )
        )
    for copy in copies:
        copy.start()

    def scan_columns(which, count):
        def step(block, slot):
            flag = structure[which, col * COL_BLOCKS + block]

            @pl.when(flag == 1)
            def _():
                blocks[slot] = block

            return slot + flag

        return lax.fori_loop(0, COL_BLOCKS, step, count)

    def scan_rows(which):
        def step(block, slot):
            flag = structure[which, row * TILE_BLOCKS + block]

            @pl.when(flag == 1)
            def _():
                rows[which, slot] = block

            return slot + flag

        used = lax.fori_loop(0, TILE_BLOCKS, step, 0)

        def pad(at, _):
            rows[which, at] = TILE_BLOCKS
            return 0

        lax.fori_loop(used, TILE_BLOCKS, pad, 0)
        return used

    parents = scan_columns(0, 0)
    both = scan_columns(1, parents)
    parent_lines, child_lines = scan_rows(0), scan_rows(1)
    first = SLOTS * turn[0]
    last = first + SLOTS
    parent_begin, parent_end = jnp.minimum(first, parents), jnp.minimum(last, parents)
    child_begin = jnp.clip(first, parents, both)
    child_end = jnp.clip(last, parents, both)
    parent_steps = (parent_end - parent_begin + 1) // 2
    steps = parent_steps + (child_end - child_begin + 1) // 2

    def slots_of(step):
        is_child = step >= parent_steps
        slot = jnp.where(is_child, child_begin + 2 * (step - parent_steps), parent_begin + 2 * step)
        return slot, jnp.where(is_child, child_end, parent_end)

    def tile_copies(step):
        slot, end = slots_of(step)
        buffer = step % 2
        copies = []
        for at in range(2):
            block = blocks[jnp.minimum(slot + at, end - 1)]
            copies.append(
                pltpu.make_async_copy(
                    parts.at[block],
                    left.at[buffer, :, :, pl.ds(2 * at * BLK, 2 * BLK)],
                    tile_sems.at[buffer, at],
                )
            )
        return copies

    for ahead in range(2):

        @pl.when(ahead < steps)
        def _():
            for copy in tile_copies(ahead):
                copy.start()

    @pl.when(turn[0] == 0)
    def _():
        acc[...] = jnp.zeros_like(acc)

    @pl.when(turn[0] > 0)
    def _():
        old = pltpu.make_async_copy(whole_old, acc.at[:, pl.ds(0, TILE_BLOCKS)], out_sem.at[0])
        old.start()
        old.wait()

    panel[SLOTS] = jnp.zeros((BLK // SUB, SUB, W), jnp.float32)
    for copy in copies[: len(pieces)]:
        copy.wait()

    def contract(which, lines, step):
        for copy in tile_copies(step):
            copy.wait()
        buffer = step % 2
        slot, end = slots_of(step)
        for at in range(2):
            here = jnp.where(slot + at < end, slot + at - first, SLOTS)
            high, low = split(panel[here].reshape(BLK, W))
            right[pl.ds(2 * at * BLK, BLK)] = high
            right[pl.ds((2 * at + 1) * BLK, BLK)] = high
            right[pl.ds((4 + at) * BLK, BLK)] = low

        for stop, chosen in ((FEW, lines <= FEW), (TILE_BLOCKS, lines > FEW)):

            @pl.when(chosen)
            def _():
                picked = [rows[which, at] for at in range(stop)]
                value = jnp.concatenate(
                    [left[buffer, jnp.minimum(at, TILE_BLOCKS - 1)] for at in picked], axis=0
                )
                value = jnp.concatenate(
                    [value, value[:, :BLK], value[:, 2 * BLK : 3 * BLK]], axis=1
                )
                part = jnp.dot(value, right[...], preferred_element_type=jnp.float32)
                for index, at in enumerate(picked):
                    acc[which, at] += part[index * BLK : (index + 1) * BLK]

        @pl.when(step + 2 < steps)
        def _():
            for copy in tile_copies(step + 2):
                copy.start()

    flat = acc.reshape(2, (TILE_BLOCKS + 1) * BLK, W)
    out_copies = []
    for which in range(2):
        made = [(acc.at[which, pl.ds(0, TILE_BLOCKS)], whole.at[which])]
        for at in range(SIDE):
            level = (z + at) % SIDE
            for ref, side in ((mine, core), (theirs, 1 - core)):
                start = pl.multiple_of((level * CORES + side) * GROUP, 32)
                made.append((flat.at[which, pl.ds(start, GROUP)], ref.at[at, :, pl.ds(which * W, W)]))
        out_copies.append(
            [
                pltpu.make_async_copy(source, to, out_sem.at[len(made) * which + at])
                for at, (source, to) in enumerate(made)
            ]
        )

    def parent_step(step, _):
        contract(0, parent_lines, step)
        return 0

    def child_step(step, _):
        contract(1, child_lines, step)
        return 0

    early_steps = jnp.minimum(parent_steps, EARLY // 2)
    lax.fori_loop(0, early_steps, parent_step, 0)
    for copy in copies[len(pieces) :]:
        copy.wait()
    lax.fori_loop(early_steps, parent_steps, parent_step, 0)
    for copy in out_copies[0]:
        copy.start()
    lax.fori_loop(parent_steps, steps, child_step, 0)
    for copy in out_copies[1]:
        copy.start()
    for copy in out_copies[0] + out_copies[1]:
        copy.wait()


def tile_products(turn, structure, parts, lines, old):
    hbm = pl.BlockSpec(memory_space=pl.ANY)
    smem = pl.BlockSpec(memory_space=pltpu.SMEM)
    return pl.pallas_call(
        tile_body,
        in_specs=[smem, smem] + [hbm] * 9,
        out_specs=[hbm] * 3,
        out_shape=[jax.ShapeDtypeStruct(array.shape, array.dtype) for array in old],
        input_output_aliases={8: 0, 9: 1, 10: 2},
        scratch_shapes=[
            pltpu.SMEM((2 * COL_BLOCKS,), jnp.int32),
            pltpu.SMEM((2, TILE_BLOCKS), jnp.int32),
            pltpu.VMEM((2, TILE_BLOCKS, BLK, 4 * BLK), jnp.bfloat16),
            pltpu.VMEM((SLOTS + 1, BLK // SUB, SUB, W), jnp.float32),
            pltpu.VMEM((6 * BLK, W), jnp.bfloat16),
            pltpu.VMEM((2, TILE_BLOCKS + 1, BLK, W), jnp.float32),
            pltpu.SemaphoreType.DMA((32,)),
            pltpu.SemaphoreType.DMA((2, 2)),
            pltpu.SemaphoreType.DMA((18,)),
        ],
        name="tile_products",
    )(
        turn,
        structure,
        parts.reshape(COL_BLOCKS, TILE_BLOCKS, BLK, 2 * BLK),
        *lines,
        *old,
    )


def ring_sum(piece, axis):
    got = []
    for at in (1, 2, 3):
        got.append(shift(piece(at), axis, at))
    return piece(0) + got[0] + got[1] + got[2]


def finish_body(base, kept, got, parent_diag, child_top, child_diag):
    half = W // CORES
    first = lax.axis_index("col") % CORES == 0
    left = jnp.where(first, kept[...], got[...])
    right = jnp.where(first, got[...], kept[...])
    for at, out in enumerate((parent_diag, child_top, child_diag)):
        columns = slice(at * half, (at + 1) * half)
        total = base[:, at * W : (at + 1) * W] + jnp.concatenate(
            [left[:, columns], right[:, columns]], axis=1
        )
        out[...] = -total if at == 1 else total


def finish(base, kept, got):
    vmem = pl.BlockSpec(memory_space=pltpu.VMEM)
    return pl.pallas_call(
        finish_body,
        in_specs=[vmem] * 3,
        out_specs=[vmem] * 3,
        out_shape=[jax.ShapeDtypeStruct((base.shape[0], W), jnp.float32)] * 3,
        name="finish",
    )(base, kept, got)


def final_sums(terms, chunks, up, down, y, x, z, core):
    half = W // CORES

    def columns(side):
        return jnp.concatenate(
            [lax.dynamic_slice_in_dim(term, side * half, half, 1) for term in terms], axis=1
        )

    def take(array, at, dim):
        return lax.dynamic_index_in_dim(array, at % SIDE, dim, keepdims=False)

    cut = chunks.shape[1] // 2
    got = lax.ppermute(columns(1 - core), AXES, PARTNER)
    value = columns(core) + got
    cube = value.reshape(SIDE, SIDE, SIDE, SUB, len(terms) * half)
    above = jnp.concatenate([chunks[1, :cut] + up, chunks[1, cut:]])
    below = jnp.concatenate([chunks[3, :cut], chunks[3, cut:] + down])
    above = shift(above, "zz", 1)
    below = shift(below, "zz", -1)
    flat = ring_sum(
        lambda at: jnp.where(core == 0, take(cube, y + at, 0), take(cube, x + at, 1)), "yx"
    )
    line = ring_sum(lambda at: take(flat, jnp.where(core == 0, x, y) + at, 0), "xy")
    value = ring_sum(lambda at: take(line, z + at, 0), "zz")
    value, above, below = lax.optimization_barrier((value, above, below))
    rows = chunks[0] + above + below
    low, high = value[: SUB // 2], value[SUB // 2 :]
    kept = jnp.where(core == 0, low, high)
    got = lax.ppermute(jnp.where(core == 0, high, low), AXES, PARTNER)
    return rows, kept, got


def invert(
    ancestor_inverse, panel_parent, panel_child, coupling, diag_parent, diag_child, structure
):
    row = lax.axis_index("row")
    col = lax.axis_index("col")
    y, x, z, core = row // SIDE, row % SIDE, col // CORES, col % CORES
    tile_rows = panel_parent.shape[0]
    group_rows = tile_rows // (SIDE * CORES)
    own_count = W // (RING * SIDE * CORES)
    own_start = (row * SIDE * CORES + col) * own_count

    panels = jnp.stack([panel_parent, panel_child]).reshape(2, TILE_BLOCKS, BLK // SUB, SUB, W)

    def slices(flip):
        to_y, to_x, _, _ = spread_target(y, x, z, core, flip)
        return lax.dynamic_index_in_dim(panels, to_y * SIDE + to_x, 2, keepdims=False)

    first = lax.ppermute(slices(0), AXES, SPREAD[0])
    second = lax.ppermute(slices(1), AXES, SPREAD[1])
    counts = structure.reshape(2, SIDE * CORES, COL_BLOCKS).sum(axis=(0, 2))
    turns = (jnp.max(counts) + SLOTS - 1) // SLOTS

    def own_rows(values):
        return lax.dynamic_slice_in_dim(values, own_start, own_count, 0)

    def base_of(coupling, diag_parent, diag_child):
        top = product(diag_parent, coupling)
        columns = lax.dynamic_slice_in_dim(coupling, own_start, own_count, 1)
        rest = own_rows(diag_child) + product_t(columns, top)
        return jnp.concatenate([own_rows(diag_parent), own_rows(top), rest], axis=1)

    def one_turn(at, old):
        turn = jnp.reshape(at, (1,))
        share = compact(turn, structure, first, second)
        share, *small = lax.optimization_barrier((share, coupling, diag_parent, diag_child))
        line = jnp.stack(gather_line(share, "xy"))
        near = gather_near(line, "yx")
        near, parts, base = lax.optimization_barrier(
            (near, narrow(ancestor_inverse), base_of(*small))
        )
        lines = (line, *near, *gather_far(*near, "yx"))
        return base, *tile_products(turn, structure, parts, lines, old[1:])

    start = tuple(
        blank((own_count, 3 * W), (2, TILE_BLOCKS, BLK, W), (SIDE, GROUP, 2 * W), (SIDE, GROUP, 2 * W))
    )
    base, whole, mine, theirs = lax.fori_loop(0, turns, one_turn, start)
    parent_whole = whole[0].reshape(tile_rows, W)
    child_whole = whole[1].reshape(tile_rows, W)

    flags = lax.dynamic_slice_in_dim(structure[1], row * TILE_BLOCKS, TILE_BLOCKS)
    block_rows = jnp.arange(tile_rows, dtype=jnp.int32)[:, None] // BLK
    hits = (block_rows == jnp.arange(TILE_BLOCKS, dtype=jnp.int32)[None, :]) & (flags[None, :] == 1)
    mask_child = jnp.any(hits, axis=1)[:, None]
    child = jnp.where(mask_child, panel_child, 0)
    mask_group = lax.dynamic_slice_in_dim(mask_child, col * group_rows, group_rows, 0)

    chunks = mine + lax.ppermute(theirs, AXES, PARTNER)
    cut = GROUP // 2
    up = shift(chunks[2, :cut], "zz", 1)
    down = shift(chunks[2, cut:], "zz", -1)
    parent_term = product_t(panel_parent, parent_whole)
    cross = product_t(parent_whole, child)
    top_term = product(parent_term, coupling) - cross
    child_term = (
        product_t(coupling, top_term) - product_t(cross, coupling) + product_t(panel_child, child_whole)
    )
    rows, kept, got = final_sums(
        [parent_term, top_term, child_term], chunks, up, down, y, x, z, core
    )
    parent_rows = -rows[:, :W]
    child_rows = -(rows[:, W:] + jnp.where(mask_group, product(parent_rows, coupling), 0))
    parent_diag, child_top, child_diag = finish(base, kept, got)
    return parent_rows, parent_diag, child_top, child_rows, child_diag


def solution(mesh):
    return jax.shard_map(
        invert,
        mesh=mesh,
        in_specs=(P("row", "col"), P("row", None), P("row", None), P(), P(), P(), P()),
        out_specs=(P(AXES, None),) * 5,
        check_vma=False,
    )
```
